32 devices in a mesh: member: 4 (over y, x), space: 8 (over z, core).
Axes of the slice: x: 2, y: 2, z: 4, core: 2. Of those that a mesh axis runs over, the one named last changes fastest.
Arguments:
- features: bfloat16 [8, 32, 64, 1024], P('member', None, 'space'), may hold values from -6 to 6
- skip: bfloat16 [8, 32, 64, 1024], P('member', None, 'space'), may hold values from -6 to 6
- conv_weight: bfloat16 [3, 3, 32, 32], replicated, may hold values from -0.625 to 0.625
- out_weight: bfloat16 [2, 32], replicated, may hold values from -2 to 2
- target: float32 [2, 64, 1024], P(None, 'space'), may hold values from -12 to 12
Outputs:
- grad_input: bfloat16 [8, 32, 64, 1024], P('member', None, 'space')
The draws below stay inside these ranges and needn't reach their ends.
All inputs are finite; a program needn't handle non-finite values.
Results may differ from the reference program's by a relative error of at most 0.012.
Values may be sent and summed in bfloat16 or wider, within the bound.
A program may use at most 64 MiB of HBM per device.

```python
import math
import jax
import jax.numpy as jnp
from jax import lax

C = 32
OUT = 2
COLS = 1024
MEMBERS = 8
ROWS = 64


def levels(stream_key, dims, cuts, smallest, top_value):
    def one(position, shards_of):
        steps = jax.random.uniform(jax.random.fold_in(jax.random.fold_in(stream_key, 6), position), (shards_of,), jnp.float32, smallest / len(cuts), top_value / len(cuts))
        return jnp.repeat(jnp.exp(steps), dims[position] // shards_of).reshape((-1,) + (1,) * (len(dims) - position - 1))

    gain = one(*cuts[0])
    for cut in cuts[1:]:
        gain = gain * one(*cut)
    return gain


def bell_draw(rng, dims, width, limit, split=(), dtype=jnp.bfloat16):
    values = width * jax.random.normal(rng, dims, jnp.float32)
    if split:
        values = values * levels(rng, dims, split, -0.22, 0.18)
    return jnp.clip(values, -limit, limit).astype(dtype)


def setup_inputs(seed: int = 0) -> dict:
    streams_of = jax.random.split(jax.random.key(seed), 6)
    features = bell_draw(streams_of[0], (MEMBERS, C, ROWS, COLS), 1.0, 6.0, ((0, 4), (2, 8)))
    skip = bell_draw(streams_of[1], (MEMBERS, C, ROWS, COLS), 1.0, 6.0, ((0, 4), (2, 8)))
    conv_weight = bell_draw(streams_of[2], (3, 3, C, C), (3 * C) ** -0.5, 0.625)
    out_weight = bell_draw(streams_of[3], (OUT, C), (C // 4) ** -0.5, 2.0)
    target = bell_draw(streams_of[4], (OUT, ROWS, COLS), 2.0, 12.0, ((1, 8),), jnp.float32)
    return dict(features=features, skip=skip, conv_weight=conv_weight, out_weight=out_weight, target=target)


root_coef = math.sqrt(2.0 / math.pi)
cubic_coef = 0.044715
smooth = 0.25

def gelu_value(source):
    inside = root_coef * (source + cubic_coef * source * source * source)
    return 0.5 * source * (1.0 + jnp.tanh(inside))

def gelu_slope(source):
    inside = root_coef * (source + cubic_coef * source * source * source)
    tanh_val = jnp.tanh(inside)
    return 0.5 * (1.0 + tanh_val) + 0.5 * source * (1.0 - tanh_val * tanh_val) * root_coef * (1.0 + 3.0 * cubic_coef * source * source)

def smooth_slope(source):
    return source / jnp.sqrt(source * source + smooth * smooth)

def stacked_taps(padded, row_count, col_count, flipped):
    pieces = []
    for row_tap in range(3):
        for col_tap in range(3):
            row_at = 2 - row_tap if flipped else row_tap
            col_at = 2 - col_tap if flipped else col_tap
            pieces.append(padded[:, row_at:row_at + row_count, col_at:col_at + col_count])
    return jnp.concatenate(pieces, axis=0).reshape(9 * padded.shape[0], row_count * col_count)

def conv_apply(source, weight, flipped):
    row_count, col_count = (source.shape[1], source.shape[2])
    padded = jnp.pad(source, ((0, 0), (1, 1), (1, 1)))
    if flipped:
        matrix = jnp.transpose(weight, (3, 0, 1, 2)).reshape(weight.shape[3], -1)
    else:
        matrix = jnp.transpose(weight, (2, 0, 1, 3)).reshape(weight.shape[2], -1)
    result = jnp.dot(matrix, stacked_taps(padded, row_count, col_count, flipped), preferred_element_type=jnp.float32)
    return result.reshape(matrix.shape[0], row_count, col_count)

def reference(features, skip, conv_weight, out_weight, target):
    member_total = features.shape[0]

    def forward_one(packed):
        source, bypass = packed
        preact = conv_apply(source, conv_weight, False) + bypass.astype(jnp.float32)
        active = gelu_value(preact).astype(jnp.bfloat16)
        flat = jnp.dot(out_weight, active.reshape(active.shape[0], -1), preferred_element_type=jnp.float32)
        return flat.reshape(out_weight.shape[0], active.shape[1], active.shape[2])
    outputs = lax.map(forward_one, (features, skip))

    def score_one(own_value):
        pair_term = lax.optimization_barrier(jnp.sum(smooth_slope(own_value[None] - outputs), axis=0))
        return smooth_slope(own_value - target) - pair_term / (member_total - 1)
    grad_out = lax.map(score_one, outputs).astype(jnp.bfloat16)

    def backward_one(triple):
        source, bypass, grad_member = triple
        preact = conv_apply(source, conv_weight, False) + bypass.astype(jnp.float32)
        flat = jnp.dot(out_weight.T, grad_member.reshape(grad_member.shape[0], -1), preferred_element_type=jnp.float32)
        grad_active = flat.reshape(preact.shape)
        grad_preact = (grad_active * gelu_slope(preact)).astype(jnp.bfloat16)
        return conv_apply(grad_preact, conv_weight, True).astype(jnp.bfloat16)
    return lax.map(backward_one, (features, skip, grad_out))
```

```python
import functools
import math

import jax
import jax.numpy as jnp
from jax import lax
from jax.experimental import pallas as pl
from jax.experimental.pallas import tpu as pltpu
from jax.sharding import PartitionSpec as P

root_coef = math.sqrt(2.0 / math.pi)
cubic_coef = 0.044715
smooth = 0.25
MESH = pl.DeviceIdType.MESH
F32 = jnp.float32
BF16 = jnp.bfloat16


def gelu_value(source):
    inside = root_coef * (source + cubic_coef * source * source * source)
    return 0.5 * source * (1.0 + jnp.tanh(inside))


def gelu_slope(source):
    square = source * source
    tanh_val = jnp.tanh(root_coef * (source + cubic_coef * square * source))
    return 0.5 * (1.0 + tanh_val) + 0.5 * source * (1.0 - tanh_val * tanh_val) * (
        root_coef * (1.0 + 3.0 * cubic_coef * square)
    )


def smooth_slope(source):
    return source * lax.rsqrt(source * source + smooth * smooth)


def dot(left, right):
    return lax.dot_general(left, right, (((1,), (0,)), ((), ())), preferred_element_type=F32)


def dot_nt(left, right):
    return lax.dot_general(left, right, (((1,), (1,)), ((), ())), preferred_element_type=F32)


def split_index(shape, dim, size):
    index = lax.broadcasted_iota(jnp.int32, shape, dim)
    if size & (size - 1) == 0:
        return lax.shift_right_logical(index, size.bit_length() - 1), index & (size - 1)
    return lax.div(index, size), lax.rem(index, size)


def shifted(value, step):
    count = value.shape[1]
    edge = jnp.zeros((value.shape[0], 1), value.dtype)
    if step == 1:
        return jnp.concatenate([value[:, 1:], edge], axis=1)
    return jnp.concatenate([edge, value[:, : count - 1]], axis=1)


def kernel(
    dims, x_hbm, skip_hbm, weight, out_w, target_hbm, out_hbm,
    x, skip, target, stk, hstk, pre, act, hs, hx, gs, hg, outs, ybuf, gsend, gout,
    wf, wfh, wb, wbh, wo, wot, sel, obuf,
    in_sem, out_sem, hs_sem, hx_sem, gs_sem, hg_sem, as_sem, ar_sem, bs_sem, br_sem,
):
    members, chans, rows, cols, peers, count, outn, chunk = dims
    full = chans * rows
    wide = cols // peers
    me = lax.axis_index("member")
    at = lax.axis_index("space")
    has_up = at > 0
    has_dn = at < count - 1
    up = {"space": lax.max(at - 1, 0)}
    dn = {"space": lax.min(at + 1, count - 1)}
    mine = pl.ds(pl.multiple_of(me * wide, wide), wide)

    loads = [pltpu.make_async_copy(x_hbm.at[m], x.at[m], in_sem.at[m]) for m in range(members)]
    skips = [
        pltpu.make_async_copy(skip_hbm.at[m], skip.at[m], in_sem.at[members + m])
        for m in range(members)
    ]
    tgt = pltpu.make_async_copy(target_hbm.at[:, mine], target, in_sem.at[2 * members])
    for c in loads + skips + [tgt]:
        c.start()

    barrier = pltpu.get_barrier_semaphore()
    for d in range(1, peers):
        pl.semaphore_signal(
            barrier, inc=1, device_id={"member": lax.rem(me + d, peers)}, device_id_type=MESH
        )

    @pl.when(has_up)
    def _():
        pl.semaphore_signal(barrier, inc=1, device_id=up, device_id_type=MESH)

    @pl.when(has_dn)
    def _():
        pl.semaphore_signal(barrier, inc=1, device_id=dn, device_id_type=MESH)

    chan, row = split_index((2 * chans, full), 1, rows)
    half, pick = split_index((2 * chans, full), 0, chans)
    sel[...] = (
        (chan == pick) & (row == jnp.where(half == 0, 0, rows - 1))
    ).astype(F32).astype(BF16)

    left_chan, left_row = split_index((full, chans), 0, rows)
    spread = (left_chan == lax.broadcasted_iota(jnp.int32, (full, chans), 1)).astype(F32)
    spread = spread.astype(BF16)
    _, row_a = split_index((full, full), 0, rows)
    _, row_b = split_index((full, full), 1, rows)
    gap = row_b - row_a

    def place(slot):
        shape = (chans, 6 * chans)
        return (
            lax.broadcasted_iota(jnp.int32, shape, 1)
            == lax.broadcasted_iota(jnp.int32, shape, 0) + slot * chans
        ).astype(F32).astype(BF16)

    def build(main, halo, flipped):
        edges = jnp.zeros((full, 6 * chans), F32)
        for dc in range(3):
            band = jnp.zeros((full, full), F32)
            for dr in range(3):
                tap = weight[dr, dc]
                part = (dot_nt if flipped else dot)(spread, tap).astype(BF16)
                offset = 1 - dr if flipped else dr - 1
                band = jnp.where(gap == offset, dot_nt(part, spread), band)
                if offset != 0:
                    kept = jnp.where(
                        left_row == (0 if offset < 0 else rows - 1), part.astype(F32), 0.0
                    ).astype(BF16)
                    edges = edges + dot(kept, place(2 * dc + (0 if offset < 0 else 1)))
            main[:, dc * full : (dc + 1) * full] = band.astype(BF16)
        halo[...] = edges.astype(BF16)

    build(wf, wfh, False)

    out_k, _ = split_index((outn * rows, chans), 0, rows)
    lines = jnp.zeros((outn * rows, chans), F32)
    for k in range(outn):
        lines = jnp.where(out_k == k, out_w[k : k + 1, :].astype(F32), lines)
    lines = lines.astype(BF16)
    _, oa = split_index((outn * rows, full), 0, rows)
    _, ob = split_index((outn * rows, full), 1, rows)
    wo[...] = jnp.where(oa == ob, dot_nt(lines, spread), 0.0).astype(BF16)
    _, ta = split_index((full, outn * rows), 0, rows)
    _, tb = split_index((full, outn * rows), 1, rows)
    wot[...] = jnp.where(ta == tb, dot_nt(spread, lines), 0.0).astype(BF16)

    pl.semaphore_wait(
        barrier, peers - 1 + has_up.astype(jnp.int32) + has_dn.astype(jnp.int32)
    )

    def halo_copies(m, src, dst, send, recv):
        to_up = pltpu.make_async_remote_copy(
            src_ref=src.at[m, 0], dst_ref=dst.at[m, 1], send_sem=send.at[m, 0],
            recv_sem=recv.at[m, 1], device_id=up, device_id_type=MESH,
        )
        to_dn = pltpu.make_async_remote_copy(
            src_ref=src.at[m, 1], dst_ref=dst.at[m, 0], send_sem=send.at[m, 1],
            recv_sem=recv.at[m, 0], device_id=dn, device_id_type=MESH,
        )
        return to_up, to_dn

    def halo_start(m, src, dst, send, recv):
        to_up, to_dn = halo_copies(m, src, dst, send, recv)

        @pl.when(has_up)
        def _():
            to_up.start()

        @pl.when(has_dn)
        def _():
            to_dn.start()

        @pl.when(jnp.logical_not(has_up))
        def _():
            dst[m, 0] = jnp.zeros((chans, cols), BF16)

        @pl.when(jnp.logical_not(has_dn))
        def _():
            dst[m, 1] = jnp.zeros((chans, cols), BF16)

    def halo_wait(m, src, dst, send, recv, which):
        to_up, to_dn = halo_copies(m, src, dst, send, recv)

        @pl.when(has_up)
        def _():
            to_up.wait_send() if which == "send" else to_dn.wait_recv()

        @pl.when(has_dn)
        def _():
            to_dn.wait_send() if which == "send" else to_up.wait_recv()

    def send_edges(m, source, store, dst, send, recv):
        edge = dot(sel[...], source).astype(BF16)
        store[m, 0] = edge[:chans]
        store[m, 1] = edge[chans:]
        halo_start(m, store, dst, send, recv)

    def stack_halo(m, halo, order):
        both = jnp.concatenate([halo[m, 0], halo[m, 1]], axis=0)
        for slot, step in enumerate(order):
            value = both if step == 0 else shifted(both, step)
            hstk[m, slot * 2 * chans : (slot + 1) * 2 * chans, :] = value

    def stack_main(m, value, order):
        for slot, step in enumerate(order):
            stk[m, slot * full : (slot + 1) * full, :] = value if step == 0 else shifted(value, step)

    spans = [slice(n, n + chunk) for n in range(0, cols, chunk)]

    for m in range(members):
        loads[m].wait()
        send_edges(m, x[m], hs, hx, hs_sem, hx_sem)
    for m in range(members):
        stack_main(m, x[m], (-1, 0, 1))
        skips[m].wait()
        for span in spans:
            pre[m, :, span] = dot(wf[...], stk[m, :, span]) + skip[m, :, span].astype(F32)

    def scatter_copy(m, d):
        peer = lax.rem(me + d, peers)
        return pltpu.make_async_remote_copy(
            src_ref=outs.at[m, :, pl.ds(pl.multiple_of(peer * wide, wide), wide)],
            dst_ref=ybuf.at[d, m],
            send_sem=as_sem.at[m, d], recv_sem=ar_sem.at[m, d],
            device_id={"member": peer}, device_id_type=MESH,
        )

    def return_copy(d):
        peer = lax.rem(me + peers - d, peers)
        return pltpu.make_async_remote_copy(
            src_ref=gsend.at[d],
            dst_ref=gout.at[:, :, mine],
            send_sem=bs_sem.at[d], recv_sem=br_sem.at[d],
            device_id={"member": peer}, device_id_type=MESH,
        )

    for m in range(members):
        halo_wait(m, hs, hx, hs_sem, hx_sem, "recv")
        stack_halo(m, hx, (-1, 0, 1))
        for span in spans:
            total = pre[m, :, span] + dot(wfh[...], hstk[m, :, span])
            pre[m, :, span] = total
            outs[m, :, span] = dot(wo[...], gelu_value(total).astype(BF16))
        for d in range(1, peers):
            scatter_copy(m, d).start()
    for m in range(members):
        for span in spans:
            pre[m, :, span] = gelu_slope(pre[m, :, span])
    build(wb, wbh, True)

    tgt.wait()
    for m in range(members):
        for d in range(1, peers):
            scatter_copy(m, d).wait_recv()
    goal = target[...]
    values = []
    for d in range(peers):
        for m in range(members):
            values.append(outs[m, :, mine] if d == 0 else ybuf[d, m])
    total_members = len(values)
    pairs = [smooth_slope(v - v) for v in values]
    for i in range(total_members):
        for j in range(i):
            term = smooth_slope(values[i] - values[j])
            pairs[i] = pairs[i] + term
            pairs[j] = pairs[j] - term
    grads = [
        (smooth_slope(values[i] - goal) - pairs[i] / (total_members - 1)).astype(BF16)
        for i in range(total_members)
    ]
    for d in range(peers):
        for m in range(members):
            grad = grads[d * members + m]
            if d == 0:
                gout[m, :, mine] = grad
            else:
                gsend[d, m] = grad
        if d > 0:
            return_copy(d).start()
    for d in range(1, peers):
        return_copy(d).wait_recv()

    for m in range(members):
        for span in spans:
            grad = dot(wot[...], gout[m, :, span])
            act[m, :, span] = (grad * pre[m, :, span]).astype(BF16)
        send_edges(m, act[m], gs, hg, gs_sem, hg_sem)
    for m in range(members):
        stack_main(m, act[m], (1, 0, -1))
        for span in spans:
            pre[m, :, span] = dot(wb[...], stk[m, :, span])
    for m in range(members):
        halo_wait(m, gs, hg, gs_sem, hg_sem, "recv")
        stack_halo(m, hg, (1, 0, -1))
        for span in spans:
            obuf[m, :, span] = (pre[m, :, span] + dot(wbh[...], hstk[m, :, span])).astype(BF16)
        pltpu.make_async_copy(obuf.at[m], out_hbm.at[m], out_sem.at[m]).start()

    for m in range(members):
        halo_wait(m, hs, hx, hs_sem, hx_sem, "send")
        halo_wait(m, gs, hg, gs_sem, hg_sem, "send")
        for d in range(1, peers):
            scatter_copy(m, d).wait_send()
    for d in range(1, peers):
        return_copy(d).wait_send()
    for m in range(members):
        pltpu.make_async_copy(obuf.at[m], out_hbm.at[m], out_sem.at[m]).wait()


def local(features, skip, conv_weight, out_weight, target):
    members, chans, rows, cols = features.shape
    outn = out_weight.shape[0]
    peers = lax.axis_size("member")
    count = lax.axis_size("space")
    full = chans * rows
    wide = cols // peers
    chunk = min(cols, 256)
    dims = (members, chans, rows, cols, peers, count, outn, chunk)
    dma = pltpu.SemaphoreType.DMA
    anywhere = pl.BlockSpec(memory_space=pl.ANY)
    vmem = pl.BlockSpec(memory_space=pltpu.VMEM)
    result = pl.pallas_call(
        functools.partial(kernel, dims),
        out_shape=jax.ShapeDtypeStruct((members, full, cols), BF16),
        in_specs=[anywhere, anywhere, vmem, vmem, anywhere],
        out_specs=anywhere,
        scratch_shapes=[
            pltpu.VMEM((members, full, cols), BF16),
            pltpu.VMEM((members, full, cols), BF16),
            pltpu.VMEM((outn * rows, wide), F32),
            pltpu.VMEM((members, 3 * full, cols), BF16),
            pltpu.VMEM((members, 6 * chans, cols), BF16),
            pltpu.VMEM((members, full, cols), F32),
            pltpu.VMEM((members, full, cols), BF16),
            pltpu.VMEM((members, 2, chans, cols), BF16),
            pltpu.VMEM((members, 2, chans, cols), BF16),
            pltpu.VMEM((members, 2, chans, cols), BF16),
            pltpu.VMEM((members, 2, chans, cols), BF16),
            pltpu.VMEM((members, outn * rows, cols), F32),
            pltpu.VMEM((peers, members, outn * rows, wide), F32),
            pltpu.VMEM((peers, members, outn * rows, wide), BF16),
            pltpu.VMEM((members, outn * rows, cols), BF16),
            pltpu.VMEM((full, 3 * full), BF16),
            pltpu.VMEM((full, 6 * chans), BF16),
            pltpu.VMEM((full, 3 * full), BF16),
            pltpu.VMEM((full, 6 * chans), BF16),
            pltpu.VMEM((outn * rows, full), BF16),
            pltpu.VMEM((full, outn * rows), BF16),
            pltpu.VMEM((2 * chans, full), BF16),
            pltpu.VMEM((members, full, cols), BF16),
            dma((2 * members + 1,)),
            dma((members,)),
            dma((members, 2)),
            dma((members, 2)),
            dma((members, 2)),
            dma((members, 2)),
            dma((members, peers)),
            dma((members, peers)),
            dma((peers,)),
            dma((peers,)),
        ],
        compiler_params=pltpu.CompilerParams(collective_id=0, has_side_effects=True),
    )(
        features.reshape(members, full, cols),
        skip.reshape(members, full, cols),
        conv_weight,
        out_weight,
        target.reshape(outn * rows, cols),
    )
    return result.reshape(members, chans, rows, cols)


def solution(mesh):
    placed = (
        P("member", None, "space", None),
        P("member", None, "space", None),
        P(),
        P(),
        P(None, "space", None),
    )
    return jax.shard_map(
        local,
        mesh=mesh,
        in_specs=placed,
        out_specs=P("member", None, "space", None),
        check_vma=False,
    )
```

```python
import functools
import math

import jax
import jax.numpy as jnp
from jax import lax
from jax.experimental import pallas as pl
from jax.experimental.pallas import tpu as pltpu
from jax.sharding import PartitionSpec as P

root_coef = math.sqrt(2.0 / math.pi)
cubic_coef = 0.044715
smooth = 0.25
MESH = pl.DeviceIdType.MESH
F32 = jnp.float32
BF16 = jnp.bfloat16


def gelu_half(source, square):
    return 0.5 + 0.5 * jnp.tanh(source * (root_coef + (root_coef * cubic_coef) * square))


def gelu_value(source):
    return source * gelu_half(source, source * source)


def gelu_slope(source):
    square = source * source
    half = gelu_half(source, square)
    rate = 2.0 * root_coef + (6.0 * root_coef * cubic_coef) * square
    return half + (source * half) * ((1.0 - half) * rate)


def smooth_slope(source):
    return source * lax.rsqrt(source * source + smooth * smooth)


def dot(left, right):
    return lax.dot_general(left, right, (((1,), (0,)), ((), ())), preferred_element_type=F32)


def dot_nt(left, right):
    return lax.dot_general(left, right, (((1,), (1,)), ((), ())), preferred_element_type=F32)


def split_index(shape, dim, size):
    index = lax.broadcasted_iota(jnp.int32, shape, dim)
    if size & (size - 1) == 0:
        return lax.shift_right_logical(index, size.bit_length() - 1), index & (size - 1)
    return lax.div(index, size), lax.rem(index, size)


def shifted(value, step):
    count = value.shape[1]
    edge = jnp.zeros((value.shape[0], 1), value.dtype)
    if step == 1:
        return jnp.concatenate([value[:, 1:], edge], axis=1)
    return jnp.concatenate([edge, value[:, : count - 1]], axis=1)


def kernel(
    dims, x_hbm, skip_hbm, weight, out_w, target_hbm, out,
    x, skip, target, stk, hstk, pre, act, hs, hx, gs, hg, outs, ybuf, gsend, gout,
    wf, wfh, wb, wbh, wo, wot, sel,
    in_sem, hs_sem, hx_sem, gs_sem, hg_sem, as_sem, ar_sem, bs_sem, br_sem,
):
    members, chans, rows, cols, peers, count, outn, chunk = dims
    full = chans * rows
    wide = cols // peers
    me = lax.axis_index("member")
    at = lax.axis_index("space")
    has_up = at > 0
    has_dn = at < count - 1
    up = {"space": lax.max(at - 1, 0)}
    dn = {"space": lax.min(at + 1, count - 1)}
    mine = pl.ds(pl.multiple_of(me * wide, wide), wide)

    loads = [pltpu.make_async_copy(x_hbm.at[m], x.at[m], in_sem.at[m]) for m in range(members)]
    skips = [
        pltpu.make_async_copy(skip_hbm.at[m], skip.at[m], in_sem.at[members + m])
        for m in range(members)
    ]
    tgt = pltpu.make_async_copy(target_hbm.at[:, mine], target, in_sem.at[2 * members])
    for c in loads + skips + [tgt]:
        c.start()

    barrier = pltpu.get_barrier_semaphore()
    for d in range(1, peers):
        pl.semaphore_signal(
            barrier, inc=1, device_id={"member": lax.rem(me + d, peers)}, device_id_type=MESH
        )

    @pl.when(has_up)
    def _():
        pl.semaphore_signal(barrier, inc=1, device_id=up, device_id_type=MESH)

    @pl.when(has_dn)
    def _():
        pl.semaphore_signal(barrier, inc=1, device_id=dn, device_id_type=MESH)

    chan, row = split_index((2 * chans, full), 1, rows)
    half, pick = split_index((2 * chans, full), 0, chans)
    sel[...] = (
        (chan == pick) & (row == jnp.where(half == 0, 0, rows - 1))
    ).astype(F32).astype(BF16)

    left_chan, left_row = split_index((full, chans), 0, rows)
    spread = (left_chan == lax.broadcasted_iota(jnp.int32, (full, chans), 1)).astype(F32)
    spread = spread.astype(BF16)
    _, row_a = split_index((full, full), 0, rows)
    _, row_b = split_index((full, full), 1, rows)
    gap = row_b - row_a

    def place(slot):
        shape = (chans, 6 * chans)
        return (
            lax.broadcasted_iota(jnp.int32, shape, 1)
            == lax.broadcasted_iota(jnp.int32, shape, 0) + slot * chans
        ).astype(F32).astype(BF16)

    def build(main, halo, flipped):
        edges = jnp.zeros((full, 6 * chans), F32)
        for dc in range(3):
            band = jnp.zeros((full, full), F32)
            for dr in range(3):
                tap = weight[dr, dc]
                part = (dot_nt if flipped else dot)(spread, tap).astype(BF16)
                offset = 1 - dr if flipped else dr - 1
                band = jnp.where(gap == offset, dot_nt(part, spread), band)
                if offset != 0:
                    kept = jnp.where(
                        left_row == (0 if offset < 0 else rows - 1), part.astype(F32), 0.0
                    ).astype(BF16)
                    edges = edges + dot(kept, place(2 * dc + (0 if offset < 0 else 1)))
            main[:, dc * full : (dc + 1) * full] = band.astype(BF16)
        halo[...] = edges.astype(BF16)

    pl.semaphore_wait(
        barrier, peers - 1 + has_up.astype(jnp.int32) + has_dn.astype(jnp.int32)
    )

    def halo_copies(m, src, dst, send, recv):
        to_up = pltpu.make_async_remote_copy(
            src_ref=src.at[m, 0], dst_ref=dst.at[m, 1], send_sem=send.at[m, 0],
            recv_sem=recv.at[m, 1], device_id=up, device_id_type=MESH,
        )
        to_dn = pltpu.make_async_remote_copy(
            src_ref=src.at[m, 1], dst_ref=dst.at[m, 0], send_sem=send.at[m, 1],
            recv_sem=recv.at[m, 0], device_id=dn, device_id_type=MESH,
        )
        return to_up, to_dn

    def halo_start(m, src, dst, send, recv):
        to_up, to_dn = halo_copies(m, src, dst, send, recv)

        @pl.when(has_up)
        def _():
            to_up.start()

        @pl.when(has_dn)
        def _():
            to_dn.start()

        @pl.when(jnp.logical_not(has_up))
        def _():
            dst[m, 0] = jnp.zeros((chans, cols), BF16)

        @pl.when(jnp.logical_not(has_dn))
        def _():
            dst[m, 1] = jnp.zeros((chans, cols), BF16)

    def halo_wait(m, src, dst, send, recv, which):
        to_up, to_dn = halo_copies(m, src, dst, send, recv)

        @pl.when(has_up)
        def _():
            to_up.wait_send() if which == "send" else to_dn.wait_recv()

        @pl.when(has_dn)
        def _():
            to_dn.wait_send() if which == "send" else to_up.wait_recv()

    def send_edges(m, source, store, dst, send, recv):
        edge = dot(sel[...], source).astype(BF16)
        store[m, 0] = edge[:chans]
        store[m, 1] = edge[chans:]
        halo_start(m, store, dst, send, recv)

    def stack_halo(m, halo, order):
        both = jnp.concatenate([halo[m, 0], halo[m, 1]], axis=0)
        for slot, step in enumerate(order):
            value = both if step == 0 else shifted(both, step)
            hstk[m, slot * 2 * chans : (slot + 1) * 2 * chans, :] = value

    def stack_main(m, value, order):
        for slot, step in enumerate(order):
            stk[m, slot * full : (slot + 1) * full, :] = value if step == 0 else shifted(value, step)

    spans = [slice(n, n + chunk) for n in range(0, cols, chunk)]

    for m in range(members):
        loads[m].wait()
        send_edges(m, x[m], hs, hx, hs_sem, hx_sem)
    build(wf, wfh, False)

    out_k, _ = split_index((outn * rows, chans), 0, rows)
    lines = jnp.zeros((outn * rows, chans), F32)
    for k in range(outn):
        lines = jnp.where(out_k == k, out_w[k : k + 1, :].astype(F32), lines)
    lines = lines.astype(BF16)
    _, oa = split_index((outn * rows, full), 0, rows)
    _, ob = split_index((outn * rows, full), 1, rows)
    wo[...] = jnp.where(oa == ob, dot_nt(lines, spread), 0.0).astype(BF16)
    _, ta = split_index((full, outn * rows), 0, rows)
    _, tb = split_index((full, outn * rows), 1, rows)
    wot[...] = jnp.where(ta == tb, dot_nt(spread, lines), 0.0).astype(BF16)
    for m in range(members):
        stack_main(m, x[m], (-1, 0, 1))
        skips[m].wait()
        for span in spans:
            pre[m, :, span] = dot(wf[...], stk[m, :, span]) + skip[m, :, span].astype(F32)

    def scatter_copy(m, d):
        peer = lax.rem(me + d, peers)
        return pltpu.make_async_remote_copy(
            src_ref=outs.at[m, :, pl.ds(pl.multiple_of(peer * wide, wide), wide)],
            dst_ref=ybuf.at[d, m],
            send_sem=as_sem.at[m, d], recv_sem=ar_sem.at[m, d],
            device_id={"member": peer}, device_id_type=MESH,
        )

    def return_copy(d):
        peer = lax.rem(me + peers - d, peers)
        return pltpu.make_async_remote_copy(
            src_ref=gsend.at[d],
            dst_ref=gout.at[:, :, mine],
            send_sem=bs_sem.at[d], recv_sem=br_sem.at[d],
            device_id={"member": peer}, device_id_type=MESH,
        )

    for m in range(members):
        halo_wait(m, hs, hx, hs_sem, hx_sem, "recv")
        stack_halo(m, hx, (-1, 0, 1))
        for span in spans:
            total = pre[m, :, span] + dot(wfh[...], hstk[m, :, span])
            pre[m, :, span] = total
            outs[m, :, span] = dot(wo[...], gelu_value(total).astype(BF16))
        for d in range(1, peers):
            scatter_copy(m, d).start()
    for m in range(members):
        for span in spans:
            pre[m, :, span] = gelu_slope(pre[m, :, span])
    tgt.wait()
    for m in range(members):
        for d in range(1, peers):
            scatter_copy(m, d).wait_recv()
    goal = target[...]
    values = []
    for d in range(peers):
        for m in range(members):
            values.append(outs[m, :, mine] if d == 0 else ybuf[d, m])
    total_members = len(values)
    pairs = [smooth_slope(v - v) for v in values]
    for i in range(total_members):
        for j in range(i):
            term = smooth_slope(values[i] - values[j])
            pairs[i] = pairs[i] + term
            pairs[j] = pairs[j] - term
    grads = [
        (smooth_slope(values[i] - goal) - pairs[i] / (total_members - 1)).astype(BF16)
        for i in range(total_members)
    ]
    for d in range(peers):
        for m in range(members):
            grad = grads[d * members + m]
            if d == 0:
                gout[m, :, mine] = grad
            else:
                gsend[d, m] = grad
        if d > 0:
            return_copy(d).start()
    build(wb, wbh, True)
    for d in range(1, peers):
        return_copy(d).wait_recv()

    for m in range(members):
        for span in spans:
            grad = dot(wot[...], gout[m, :, span])
            act[m, :, span] = (grad * pre[m, :, span]).astype(BF16)
        send_edges(m, act[m], gs, hg, gs_sem, hg_sem)
    for m in range(members):
        stack_main(m, act[m], (1, 0, -1))
        for span in spans:
            pre[m, :, span] = dot(wb[...], stk[m, :, span])
    for m in range(members):
        halo_wait(m, gs, hg, gs_sem, hg_sem, "recv")
        stack_halo(m, hg, (1, 0, -1))
        for span in spans:
            out[m, :, span] = (pre[m, :, span] + dot(wbh[...], hstk[m, :, span])).astype(BF16)

    for m in range(members):
        halo_wait(m, hs, hx, hs_sem, hx_sem, "send")
        halo_wait(m, gs, hg, gs_sem, hg_sem, "send")
        for d in range(1, peers):
            scatter_copy(m, d).wait_send()
    for d in range(1, peers):
        return_copy(d).wait_send()


def local(features, skip, conv_weight, out_weight, target):
    members, chans, rows, cols = features.shape
    outn = out_weight.shape[0]
    peers = lax.axis_size("member")
    count = lax.axis_size("space")
    full = chans * rows
    wide = cols // peers
    chunk = min(cols, 256)
    dims = (members, chans, rows, cols, peers, count, outn, chunk)
    dma = pltpu.SemaphoreType.DMA
    anywhere = pl.BlockSpec(memory_space=pltpu.HBM)
    vmem = pl.BlockSpec(memory_space=pltpu.VMEM)
    result = pl.pallas_call(
        functools.partial(kernel, dims),
        out_shape=pltpu.VMEM((members, full, cols), BF16),
        in_specs=[anywhere, anywhere, vmem, vmem, anywhere],
        out_specs=vmem,
        scratch_shapes=[
            pltpu.VMEM((members, full, cols), BF16),
            pltpu.VMEM((members, full, cols), BF16),
            pltpu.VMEM((outn * rows, wide), F32),
            pltpu.VMEM((members, 3 * full, cols), BF16),
            pltpu.VMEM((members, 6 * chans, cols), BF16),
            pltpu.VMEM((members, full, cols), F32),
            pltpu.VMEM((members, full, cols), BF16),
            pltpu.VMEM((members, 2, chans, cols), BF16),
            pltpu.VMEM((members, 2, chans, cols), BF16),
            pltpu.VMEM((members, 2, chans, cols), BF16),
            pltpu.VMEM((members, 2, chans, cols), BF16),
            pltpu.VMEM((members, outn * rows, cols), F32),
            pltpu.VMEM((peers, members, outn * rows, wide), F32),
            pltpu.VMEM((peers, members, outn * rows, wide), BF16),
            pltpu.VMEM((members, outn * rows, cols), BF16),
            pltpu.VMEM((full, 3 * full), BF16),
            pltpu.VMEM((full, 6 * chans), BF16),
            pltpu.VMEM((full, 3 * full), BF16),
            pltpu.VMEM((full, 6 * chans), BF16),
            pltpu.VMEM((outn * rows, full), BF16),
            pltpu.VMEM((full, outn * rows), BF16),
            pltpu.VMEM((2 * chans, full), BF16),
            dma((2 * members + 1,)),
            dma((members, 2)),
            dma((members, 2)),
            dma((members, 2)),
            dma((members, 2)),
            dma((members, peers)),
            dma((members, peers)),
            dma((peers,)),
            dma((peers,)),
        ],
        compiler_params=pltpu.CompilerParams(collective_id=0, has_side_effects=True, vmem_limit_bytes=58 * 2**20),
    )(
        features.reshape(members, full, cols),
        skip.reshape(members, full, cols),
        conv_weight,
        out_weight,
        target.reshape(outn * rows, cols),
    )
    return result.reshape(members, chans, rows, cols)


def solution(mesh):
    placed = (
        P("member", None, "space", None),
        P("member", None, "space", None),
        P(),
        P(),
        P(None, "space", None),
    )
    return jax.shard_map(
        local,
        mesh=mesh,
        in_specs=placed,
        out_specs=P("member", None, "space", None),
        check_vma=False,
    )
```

```python
import functools
import math

import jax
import jax.numpy as jnp
from jax import lax
from jax.experimental import pallas as pl
from jax.experimental.pallas import tpu as pltpu
from jax.sharding import PartitionSpec as P

root_coef = math.sqrt(2.0 / math.pi)
cubic_coef = 0.044715
smooth = 0.25
lane = 128
MESH = pl.DeviceIdType.MESH
F32 = jnp.float32
BF16 = jnp.bfloat16


def gelu_half(source, square):
    return 0.5 + 0.5 * jnp.tanh(source * (root_coef + (root_coef * cubic_coef) * square))


def gelu_value(source):
    return source * gelu_half(source, source * source)


def gelu_slope(source):
    square = source * source
    half = gelu_half(source, square)
    rate = 2.0 * root_coef + (6.0 * root_coef * cubic_coef) * square
    return half + (source * half) * ((1.0 - half) * rate)


def smooth_slope(source):
    return source * lax.rsqrt(source * source + smooth * smooth)


def dot(left, right):
    return lax.dot_general(left, right, (((1,), (0,)), ((), ())), preferred_element_type=F32)


def dot_nt(left, right):
    return lax.dot_general(left, right, (((1,), (1,)), ((), ())), preferred_element_type=F32)


def split_index(shape, dim, size):
    index = lax.broadcasted_iota(jnp.int32, shape, dim)
    if size & (size - 1) == 0:
        return lax.shift_right_logical(index, size.bit_length() - 1), index & (size - 1)
    return lax.div(index, size), lax.rem(index, size)


def shifted(value, step):
    count = value.shape[1]
    edge = jnp.zeros((value.shape[0], 1), value.dtype)
    if step == 1:
        return jnp.concatenate([value[:, 1:], edge], axis=1)
    return jnp.concatenate([edge, value[:, : count - 1]], axis=1)


def kernel(
    dims, x_hbm, skip_hbm, weight, out_w, target_hbm, out,
    x, skip, target, stk, hstk, pre, act, hs, hx, gs, hg, outs, osend, ybuf, gout, se, woe,
    wf, wfh, wb, wbh, wo, wot, sel,
    in_sem, hs_sem, hx_sem, gs_sem, hg_sem, as_sem, ar_sem,
):
    members, chans, rows, cols, peers, count, outn, chunk = dims
    full = chans * rows
    me = lax.axis_index("member")
    at = lax.axis_index("space")
    has_up = at > 0
    has_dn = at < count - 1
    up = {"space": lax.max(at - 1, 0)}
    dn = {"space": lax.min(at + 1, count - 1)}

    loads = [pltpu.make_async_copy(x_hbm.at[m], x.at[m], in_sem.at[m]) for m in range(members)]
    skips = [
        pltpu.make_async_copy(skip_hbm.at[m], skip.at[m], in_sem.at[members + m])
        for m in range(members)
    ]
    tgt = pltpu.make_async_copy(target_hbm, target, in_sem.at[2 * members])
    for c in loads + skips + [tgt]:
        c.start()

    barrier = pltpu.get_barrier_semaphore()
    for d in range(1, peers):
        pl.semaphore_signal(
            barrier, inc=1, device_id={"member": lax.rem(me + d, peers)}, device_id_type=MESH
        )

    @pl.when(has_up)
    def _():
        pl.semaphore_signal(barrier, inc=1, device_id=up, device_id_type=MESH)

    @pl.when(has_dn)
    def _():
        pl.semaphore_signal(barrier, inc=1, device_id=dn, device_id_type=MESH)

    chan, row = split_index((2 * chans, full), 1, rows)
    half, pick = split_index((2 * chans, full), 0, chans)
    sel[...] = (
        (chan == pick) & (row == jnp.where(half == 0, 0, rows - 1))
    ).astype(F32).astype(BF16)

    left_chan, left_row = split_index((full, chans), 0, rows)
    spread = (left_chan == lax.broadcasted_iota(jnp.int32, (full, chans), 1)).astype(F32)
    spread = spread.astype(BF16)
    _, row_a = split_index((full, full), 0, rows)
    _, row_b = split_index((full, full), 1, rows)
    gap = row_b - row_a

    def place(slot):
        shape = (chans, 6 * chans)
        return (
            lax.broadcasted_iota(jnp.int32, shape, 1)
            == lax.broadcasted_iota(jnp.int32, shape, 0) + slot * chans
        ).astype(F32).astype(BF16)

    def build(main, halo, flipped):
        edges = jnp.zeros((full, 6 * chans), F32)
        for dc in range(3):
            band = jnp.zeros((full, full), F32)
            for dr in range(3):
                offset = 1 - dr if flipped else dr - 1
                if flipped and offset == 0:
                    continue
                part = (dot_nt if flipped else dot)(spread, weight[dr, dc]).astype(BF16)
                if not flipped:
                    band = jnp.where(gap == offset, dot_nt(part, spread), band)
                if offset != 0:
                    kept = jnp.where(
                        left_row == (0 if offset < 0 else rows - 1), part.astype(F32), 0.0
                    ).astype(BF16)
                    edges = edges + dot(kept, place(2 * dc + (0 if offset < 0 else 1)))
            span = slice(dc * full, (dc + 1) * full)
            main[:, span] = wf[:, span].T if flipped else band.astype(BF16)
        halo[...] = edges.astype(BF16)

    pl.semaphore_wait(
        barrier, peers - 1 + has_up.astype(jnp.int32) + has_dn.astype(jnp.int32)
    )

    def halo_copies(m, src, dst, send, recv):
        to_up = pltpu.make_async_remote_copy(
            src_ref=src.at[m, 0], dst_ref=dst.at[m, 1], send_sem=send.at[m, 0],
            recv_sem=recv.at[m, 1], device_id=up, device_id_type=MESH,
        )
        to_dn = pltpu.make_async_remote_copy(
            src_ref=src.at[m, 1], dst_ref=dst.at[m, 0], send_sem=send.at[m, 1],
            recv_sem=recv.at[m, 0], device_id=dn, device_id_type=MESH,
        )
        return to_up, to_dn

    def halo_start(m, src, dst, send, recv):
        to_up, to_dn = halo_copies(m, src, dst, send, recv)

        @pl.when(has_up)
        def _():
            to_up.start()

        @pl.when(has_dn)
        def _():
            to_dn.start()

        @pl.when(jnp.logical_not(has_up))
        def _():
            dst[m, 0] = jnp.zeros((chans, cols), BF16)

        @pl.when(jnp.logical_not(has_dn))
        def _():
            dst[m, 1] = jnp.zeros((chans, cols), BF16)

    def halo_wait(m, src, dst, send, recv, which):
        to_up, to_dn = halo_copies(m, src, dst, send, recv)

        @pl.when(has_up)
        def _():
            to_up.wait_send() if which == "send" else to_dn.wait_recv()

        @pl.when(has_dn)
        def _():
            to_dn.wait_send() if which == "send" else to_up.wait_recv()

    def send_edges(m, source, store, dst, send, recv):
        edge = dot(sel[...], source).astype(BF16)
        store[m, 0] = edge[:chans]
        store[m, 1] = edge[chans:]
        halo_start(m, store, dst, send, recv)

    def stack_halo(m, halo, order):
        both = jnp.concatenate([halo[m, 0], halo[m, 1]], axis=0)
        for slot, step in enumerate(order):
            value = both if step == 0 else shifted(both, step)
            hstk[m, slot * 2 * chans : (slot + 1) * 2 * chans, :] = value

    def stack_main(m, value, order):
        for slot, step in enumerate(order):
            stk[m, slot * full : (slot + 1) * full, :] = value if step == 0 else shifted(value, step)

    spans = [slice(n, n + chunk) for n in range(0, cols, chunk)]

    def get(m, span, lines=slice(None)):
        tiles = range(span.start // lane, span.stop // lane)
        return jnp.concatenate([pre[m, tile, lines, :] for tile in tiles], axis=1)

    def put(m, span, value, lines=slice(None)):
        for k, tile in enumerate(range(span.start // lane, span.stop // lane)):
            pre[m, tile, lines, :] = value[:, k * lane : (k + 1) * lane]

    for m in range(members):
        loads[m].wait()
        send_edges(m, x[m], hs, hx, hs_sem, hx_sem)
    build(wf, wfh, False)

    out_k, _ = split_index((outn * rows, chans), 0, rows)
    lines = jnp.zeros((outn * rows, chans), F32)
    for k in range(outn):
        lines = jnp.where(out_k == k, out_w[k : k + 1, :].astype(F32), lines)
    lines = lines.astype(BF16)
    _, oa = split_index((outn * rows, full), 0, rows)
    _, ob = split_index((outn * rows, full), 1, rows)
    wo[...] = jnp.where(oa == ob, dot_nt(lines, spread), 0.0).astype(BF16)
    _, ta = split_index((full, outn * rows), 0, rows)
    _, tb = split_index((full, outn * rows), 1, rows)
    wot[...] = jnp.where(ta == tb, dot_nt(spread, lines), 0.0).astype(BF16)
    for m in range(members):
        stack_main(m, x[m], (-1, 0, 1))
        skips[m].wait()
        for span in spans:
            put(m, span, dot(wf[...], stk[m, :, span]) + skip[m, :, span].astype(F32))

    parts = [slice(n, n + cols // 2) for n in range(0, cols, cols // 2)]

    def gather_copy(m, part, d):
        return pltpu.make_async_remote_copy(
            src_ref=osend.at[m, :, parts[part]],
            dst_ref=ybuf.at[d, m, :, parts[part]],
            send_sem=as_sem.at[m, part, d], recv_sem=ar_sem.at[m, part, d],
            device_id={"member": lax.rem(me + d, peers)}, device_id_type=MESH,
        )

    for m in range(members):
        halo_wait(m, hs, hx, hs_sem, hx_sem, "recv")
        stack_halo(m, hx, (-1, 0, 1))
        for part, range_of in enumerate(parts):
            for n in range(range_of.start, range_of.stop, chunk):
                span = slice(n, n + chunk)
                total = get(m, span) + dot(wfh[...], hstk[m, :, span])
                put(m, span, total)
                value = dot(wo[...], gelu_value(total).astype(BF16))
                outs[m, :, span] = value
                osend[m, :, span] = value.astype(BF16)
            for d in range(1, peers):
                gather_copy(m, part, d).start()
    block = 8 * rows
    for m in range(members):
        for n in range(0, full, block):
            for span in spans:
                lines = slice(n, n + block)
                put(m, span, gelu_slope(get(m, span, lines)), lines)
        for half in range(2):
            for tile in range(cols // lane):
                kept = pre[m, tile, pl.ds(half * (rows - 1), chans, stride=rows), :]
                se[m, half, :, tile * lane : (tile + 1) * lane] = kept
    build(wb, wbh, True)
    woe[...] = dot(sel[...], wot[...]).astype(BF16)

    tgt.wait()
    total_members = peers * members
    for part in range(2):
        for d in range(1, peers):
            for m in range(members):
                gather_copy(m, part, d).wait_recv()
        for n in range(parts[part].start, parts[part].stop, chunk):
            span = slice(n, n + chunk)
            own = [outs[m, :, span] for m in range(members)]
            pairs = [smooth_slope(v - v) for v in own]
            for i in range(members):
                for j in range(i):
                    term = smooth_slope(own[i] - own[j])
                    pairs[i] = pairs[i] + term
                    pairs[j] = pairs[j] - term
            for d in range(1, peers):
                for j in range(members):
                    other = ybuf[d, j, :, span].astype(F32)
                    for i in range(members):
                        pairs[i] = pairs[i] + smooth_slope(own[i] - other)
            for i in range(members):
                gout[i, :, span] = (
                    smooth_slope(own[i] - target[:, span]) - pairs[i] / (total_members - 1)
                ).astype(BF16)

    for m in range(members):
        edge = dot(woe[...], gout[m])
        for half in range(2):
            gs[m, half] = (edge[half * chans : (half + 1) * chans] * se[m, half]).astype(BF16)
        halo_start(m, gs, hg, gs_sem, hg_sem)
    for m in range(members):
        for span in spans:
            grad = dot(wot[...], gout[m, :, span])
            act[m, :, span] = (grad * get(m, span)).astype(BF16)
    for m in range(members):
        stack_main(m, act[m], (1, 0, -1))
        for span in spans:
            put(m, span, dot(wb[...], stk[m, :, span]))
    for m in range(members):
        halo_wait(m, gs, hg, gs_sem, hg_sem, "recv")
        stack_halo(m, hg, (1, 0, -1))
        for span in spans:
            out[m, :, span] = (get(m, span) + dot(wbh[...], hstk[m, :, span])).astype(BF16)

    for m in range(members):
        halo_wait(m, hs, hx, hs_sem, hx_sem, "send")
        halo_wait(m, gs, hg, gs_sem, hg_sem, "send")
        for part in range(2):
            for d in range(1, peers):
                gather_copy(m, part, d).wait_send()


def local(features, skip, conv_weight, out_weight, target):
    members, chans, rows, cols = features.shape
    outn = out_weight.shape[0]
    peers = lax.axis_size("member")
    count = lax.axis_size("space")
    full = chans * rows
    chunk = min(cols, 256)
    dims = (members, chans, rows, cols, peers, count, outn, chunk)
    dma = pltpu.SemaphoreType.DMA
    anywhere = pl.BlockSpec(memory_space=pltpu.HBM)
    vmem = pl.BlockSpec(memory_space=pltpu.VMEM)
    result = pl.pallas_call(
        functools.partial(kernel, dims),
        out_shape=pltpu.VMEM((members, full, cols), BF16),
        in_specs=[anywhere, anywhere, vmem, vmem, anywhere],
        out_specs=vmem,
        scratch_shapes=[
            pltpu.VMEM((members, full, cols), BF16),
            pltpu.VMEM((members, full, cols), BF16),
            pltpu.VMEM((outn * rows, cols), F32),
            pltpu.VMEM((members, 3 * full, cols), BF16),
            pltpu.VMEM((members, 6 * chans, cols), BF16),
            pltpu.VMEM((members, cols // lane, full, lane), F32),
            pltpu.VMEM((members, full, cols), BF16),
            pltpu.VMEM((members, 2, chans, cols), BF16),
            pltpu.VMEM((members, 2, chans, cols), BF16),
            pltpu.VMEM((members, 2, chans, cols), BF16),
            pltpu.VMEM((members, 2, chans, cols), BF16),
            pltpu.VMEM((members, outn * rows, cols), F32),
            pltpu.VMEM((members, outn * rows, cols), BF16),
            pltpu.VMEM((peers, members, outn * rows, cols), BF16),
            pltpu.VMEM((members, outn * rows, cols), BF16),
            pltpu.VMEM((members, 2, chans, cols), F32),
            pltpu.VMEM((2 * chans, outn * rows), BF16),
            pltpu.VMEM((full, 3 * full), BF16),
            pltpu.VMEM((full, 6 * chans), BF16),
            pltpu.VMEM((full, 3 * full), BF16),
            pltpu.VMEM((full, 6 * chans), BF16),
            pltpu.VMEM((outn * rows, full), BF16),
            pltpu.VMEM((full, outn * rows), BF16),
            pltpu.VMEM((2 * chans, full), BF16),
            dma((2 * members + 1,)),
            dma((members, 2)),
            dma((members, 2)),
            dma((members, 2)),
            dma((members, 2)),
            dma((members, 2, peers)),
            dma((members, 2, peers)),
        ],
        compiler_params=pltpu.CompilerParams(collective_id=0, has_side_effects=True, vmem_limit_bytes=58 * 2**20),
    )(
        features.reshape(members, full, cols),
        skip.reshape(members, full, cols),
        conv_weight,
        out_weight,
        target.reshape(outn * rows, cols),
    )
    return result.reshape(members, chans, rows, cols)


def solution(mesh):
    placed = (
        P("member", None, "space", None),
        P("member", None, "space", None),
        P(),
        P(),
        P(None, "space", None),
    )
    return jax.shard_map(
        local,
        mesh=mesh,
        in_specs=placed,
        out_specs=P("member", None, "space", None),
        check_vma=False,
    )
```

```python
import functools
import math

import jax
import jax.numpy as jnp
from jax import lax
from jax.experimental import pallas as pl
from jax.experimental.pallas import tpu as pltpu
from jax.sharding import PartitionSpec as P

root_coef = math.sqrt(2.0 / math.pi)
cubic_coef = 0.044715
smooth = 0.25
lane = 128
MESH = pl.DeviceIdType.MESH
F32 = jnp.float32
BF16 = jnp.bfloat16


def gelu_half(source, square):
    return 0.5 + 0.5 * jnp.tanh(source * (root_coef + (root_coef * cubic_coef) * square))


def gelu_value(source):
    return source * gelu_half(source, source * source)


def gelu_slope(source):
    square = source * source
    half = gelu_half(source, square)
    rate = 2.0 * root_coef + (6.0 * root_coef * cubic_coef) * square
    return half + (source * half) * ((1.0 - half) * rate)


def smooth_slope(source):
    return source * lax.rsqrt(source * source + smooth * smooth)


def dot(left, right):
    return lax.dot_general(left, right, (((1,), (0,)), ((), ())), preferred_element_type=F32)


def dot_nt(left, right):
    return lax.dot_general(left, right, (((1,), (1,)), ((), ())), preferred_element_type=F32)


def split_index(shape, dim, size):
    index = lax.broadcasted_iota(jnp.int32, shape, dim)
    if size & (size - 1) == 0:
        return lax.shift_right_logical(index, size.bit_length() - 1), index & (size - 1)
    return lax.div(index, size), lax.rem(index, size)


def shifted(value, step):
    count = value.shape[1]
    edge = jnp.zeros((value.shape[0], 1), value.dtype)
    if step == 1:
        return jnp.concatenate([value[:, 1:], edge], axis=1)
    return jnp.concatenate([edge, value[:, : count - 1]], axis=1)


def kernel(
    dims, x_hbm, skip_hbm, weight, out_w, target_hbm, out,
    x, skip, target, stk, hstk, pre, act, hs, hx, hse, hg, hgo, outs, osend, ybuf, gout, se, woe,
    wf, wfh, wb, wbh, wo, wot, sel,
    in_sem, hs_sem, hx_sem, gs_sem, hg_sem, as_sem, ar_sem, cs_sem, cr_sem,
):
    members, chans, rows, cols, peers, count, outn, chunk = dims
    full = chans * rows
    me = lax.axis_index("member")
    at = lax.axis_index("space")
    has_up = at > 0
    has_dn = at < count - 1
    up = {"space": lax.max(at - 1, 0)}
    dn = {"space": lax.min(at + 1, count - 1)}

    loads = [pltpu.make_async_copy(x_hbm.at[m], x.at[m], in_sem.at[m]) for m in range(members)]
    skips = [
        pltpu.make_async_copy(skip_hbm.at[m], skip.at[m], in_sem.at[members + m])
        for m in range(members)
    ]
    tgt = pltpu.make_async_copy(target_hbm, target, in_sem.at[2 * members])
    for c in loads + skips + [tgt]:
        c.start()

    barrier = pltpu.get_barrier_semaphore()
    for d in range(1, peers):
        pl.semaphore_signal(
            barrier, inc=1, device_id={"member": lax.rem(me + d, peers)}, device_id_type=MESH
        )

    @pl.when(has_up)
    def _():
        pl.semaphore_signal(barrier, inc=1, device_id=up, device_id_type=MESH)

    @pl.when(has_dn)
    def _():
        pl.semaphore_signal(barrier, inc=1, device_id=dn, device_id_type=MESH)

    chan, row = split_index((2 * chans, full), 1, rows)
    half, pick = split_index((2 * chans, full), 0, chans)
    sel[...] = (
        (chan == pick) & (row == jnp.where(half == 0, 0, rows - 1))
    ).astype(F32).astype(BF16)

    left_chan, left_row = split_index((full, chans), 0, rows)
    spread = (left_chan == lax.broadcasted_iota(jnp.int32, (full, chans), 1)).astype(F32)
    spread = spread.astype(BF16)
    _, row_a = split_index((full, full), 0, rows)
    _, row_b = split_index((full, full), 1, rows)
    gap = row_b - row_a

    def place(slot):
        shape = (chans, 6 * chans)
        return (
            lax.broadcasted_iota(jnp.int32, shape, 1)
            == lax.broadcasted_iota(jnp.int32, shape, 0) + slot * chans
        ).astype(F32).astype(BF16)

    def build(main, halo, flipped):
        edges = jnp.zeros((full, 6 * chans), F32)
        for dc in range(3):
            band = jnp.zeros((full, full), F32)
            for dr in range(3):
                offset = 1 - dr if flipped else dr - 1
                if flipped and offset == 0:
                    continue
                part = (dot_nt if flipped else dot)(spread, weight[dr, dc]).astype(BF16)
                if not flipped:
                    band = jnp.where(gap == offset, dot_nt(part, spread), band)
                if offset != 0:
                    kept = jnp.where(
                        left_row == (0 if offset < 0 else rows - 1), part.astype(F32), 0.0
                    ).astype(BF16)
                    edges = edges + dot(kept, place(2 * dc + (0 if offset < 0 else 1)))
            span = slice(dc * full, (dc + 1) * full)
            main[:, span] = wf[:, span].T if flipped else band.astype(BF16)
        halo[...] = edges.astype(BF16)

    pl.semaphore_wait(
        barrier, peers - 1 + has_up.astype(jnp.int32) + has_dn.astype(jnp.int32)
    )

    def edge_of(src, m, half):
        return src.at[m, half] if len(src.shape) == 4 else src.at[m]

    def halo_copies(m, src, dst, send, recv):
        to_up = pltpu.make_async_remote_copy(
            src_ref=edge_of(src, m, 0), dst_ref=dst.at[m, 1], send_sem=send.at[m, 0],
            recv_sem=recv.at[m, 1], device_id=up, device_id_type=MESH,
        )
        to_dn = pltpu.make_async_remote_copy(
            src_ref=edge_of(src, m, 1), dst_ref=dst.at[m, 0], send_sem=send.at[m, 1],
            recv_sem=recv.at[m, 0], device_id=dn, device_id_type=MESH,
        )
        return to_up, to_dn

    def halo_start(m, src, dst, send, recv):
        to_up, to_dn = halo_copies(m, src, dst, send, recv)

        @pl.when(has_up)
        def _():
            to_up.start()

        @pl.when(has_dn)
        def _():
            to_dn.start()

        @pl.when(jnp.logical_not(has_up))
        def _():
            dst[m, 0] = jnp.zeros(dst.shape[2:], dst.dtype)

        @pl.when(jnp.logical_not(has_dn))
        def _():
            dst[m, 1] = jnp.zeros(dst.shape[2:], dst.dtype)

    def halo_wait(m, src, dst, send, recv, which):
        to_up, to_dn = halo_copies(m, src, dst, send, recv)

        @pl.when(has_up)
        def _():
            to_up.wait_send() if which == "send" else to_dn.wait_recv()

        @pl.when(has_dn)
        def _():
            to_dn.wait_send() if which == "send" else to_up.wait_recv()

    def send_edges(m, source, store, dst, send, recv):
        edge = dot(sel[...], source).astype(BF16)
        store[m, 0] = edge[:chans]
        store[m, 1] = edge[chans:]
        halo_start(m, store, dst, send, recv)

    def stack_halo(m, halo, order):
        both = jnp.concatenate([halo[m, 0], halo[m, 1]], axis=0)
        for slot, step in enumerate(order):
            value = both if step == 0 else shifted(both, step)
            hstk[m, slot * 2 * chans : (slot + 1) * 2 * chans, :] = value

    def stack_main(m, value, order):
        for slot, step in enumerate(order):
            stk[m, slot * full : (slot + 1) * full, :] = value if step == 0 else shifted(value, step)

    spans = [slice(n, n + chunk) for n in range(0, cols, chunk)]

    def get(m, span, lines=slice(None)):
        tiles = range(span.start // lane, span.stop // lane)
        return jnp.concatenate([pre[m, tile, lines, :] for tile in tiles], axis=1)

    def put(m, span, value, lines=slice(None)):
        for k, tile in enumerate(range(span.start // lane, span.stop // lane)):
            pre[m, tile, lines, :] = value[:, k * lane : (k + 1) * lane]

    for m in range(members):
        loads[m].wait()
        send_edges(m, x[m], hs, hx, hs_sem, hx_sem)
    build(wf, wfh, False)

    out_k, _ = split_index((outn * rows, chans), 0, rows)
    lines = jnp.zeros((outn * rows, chans), F32)
    for k in range(outn):
        lines = jnp.where(out_k == k, out_w[k : k + 1, :].astype(F32), lines)
    lines = lines.astype(BF16)
    _, oa = split_index((outn * rows, full), 0, rows)
    _, ob = split_index((outn * rows, full), 1, rows)
    wo[...] = jnp.where(oa == ob, dot_nt(lines, spread), 0.0).astype(BF16)
    _, ta = split_index((full, outn * rows), 0, rows)
    _, tb = split_index((full, outn * rows), 1, rows)
    wot[...] = jnp.where(ta == tb, dot_nt(spread, lines), 0.0).astype(BF16)
    for m in range(members):
        stack_main(m, x[m], (-1, 0, 1))
        skips[m].wait()
        for span in spans:
            put(m, span, dot(wf[...], stk[m, :, span]) + skip[m, :, span].astype(F32))

    parts = [slice(n, n + cols // 2) for n in range(0, cols, cols // 2)]

    def gather_copy(m, part, d):
        return pltpu.make_async_remote_copy(
            src_ref=osend.at[m, :, parts[part]],
            dst_ref=ybuf.at[d, m, :, parts[part]],
            send_sem=as_sem.at[m, part, d], recv_sem=ar_sem.at[m, part, d],
            device_id={"member": lax.rem(me + d, peers)}, device_id_type=MESH,
        )

    for m in range(members):
        halo_wait(m, hs, hx, hs_sem, hx_sem, "recv")
        stack_halo(m, hx, (-1, 0, 1))
        for part, range_of in enumerate(parts):
            for n in range(range_of.start, range_of.stop, chunk):
                span = slice(n, n + chunk)
                total = get(m, span) + dot(wfh[...], hstk[m, :, span])
                put(m, span, total)
                value = dot(wo[...], gelu_value(total).astype(BF16))
                outs[m, :, span] = value
                osend[m, :, span] = value.astype(BF16)
            for d in range(1, peers):
                gather_copy(m, part, d).start()
    block = 8 * rows
    for m in range(members):
        for n in range(0, full, block):
            for span in spans:
                lines = slice(n, n + block)
                put(m, span, gelu_slope(get(m, span, lines)), lines)
        for half in range(2):
            for tile in range(cols // lane):
                kept = pre[m, tile, pl.ds(half * (rows - 1), chans, stride=rows), :]
                se[m, half, :, tile * lane : (tile + 1) * lane] = kept
        halo_start(m, se, hse, gs_sem, hg_sem)
    build(wb, wbh, True)
    woe[...] = dot(sel[...], wot[...]).astype(BF16)

    tgt.wait()
    total_members = peers * members
    for part in range(2):
        for d in range(1, peers):
            for m in range(members):
                gather_copy(m, part, d).wait_recv()
        for n in range(parts[part].start, parts[part].stop, chunk):
            span = slice(n, n + chunk)
            own = [outs[m, :, span] for m in range(members)]
            pairs = [smooth_slope(v - v) for v in own]
            for i in range(members):
                for j in range(i):
                    term = smooth_slope(own[i] - own[j])
                    pairs[i] = pairs[i] + term
                    pairs[j] = pairs[j] - term
            for d in range(1, peers):
                for j in range(members):
                    other = ybuf[d, j, :, span].astype(F32)
                    for i in range(members):
                        pairs[i] = pairs[i] + smooth_slope(own[i] - other)
            for i in range(members):
                gout[i, :, span] = (
                    smooth_slope(own[i] - target[:, span]) - pairs[i] / (total_members - 1)
                ).astype(BF16)

    for m in range(members):
        halo_start(m, gout, hgo, cs_sem, cr_sem)
    for m in range(members):
        for span in spans:
            grad = dot(wot[...], gout[m, :, span])
            act[m, :, span] = (grad * get(m, span)).astype(BF16)
    for m in range(members):
        stack_main(m, act[m], (1, 0, -1))
        for span in spans:
            put(m, span, dot(wb[...], stk[m, :, span]))
    for m in range(members):
        halo_wait(m, se, hse, gs_sem, hg_sem, "recv")
        halo_wait(m, gout, hgo, cs_sem, cr_sem, "recv")
        for half in range(2):
            far = woe[(1 - half) * chans : (2 - half) * chans, :]
            hg[m, half] = (dot(far, hgo[m, half]) * hse[m, half]).astype(BF16)
        stack_halo(m, hg, (1, 0, -1))
        for span in spans:
            out[m, :, span] = (get(m, span) + dot(wbh[...], hstk[m, :, span])).astype(BF16)

    for m in range(members):
        halo_wait(m, hs, hx, hs_sem, hx_sem, "send")
        halo_wait(m, se, hse, gs_sem, hg_sem, "send")
        halo_wait(m, gout, hgo, cs_sem, cr_sem, "send")
        for part in range(2):
            for d in range(1, peers):
                gather_copy(m, part, d).wait_send()


def local(features, skip, conv_weight, out_weight, target):
    members, chans, rows, cols = features.shape
    outn = out_weight.shape[0]
    peers = lax.axis_size("member")
    count = lax.axis_size("space")
    full = chans * rows
    chunk = min(cols, 256)
    dims = (members, chans, rows, cols, peers, count, outn, chunk)
    dma = pltpu.SemaphoreType.DMA
    anywhere = pl.BlockSpec(memory_space=pltpu.HBM)
    vmem = pl.BlockSpec(memory_space=pltpu.VMEM)
    result = pl.pallas_call(
        functools.partial(kernel, dims),
        out_shape=pltpu.VMEM((members, full, cols), BF16),
        in_specs=[anywhere, anywhere, vmem, vmem, anywhere],
        out_specs=vmem,
        scratch_shapes=[
            pltpu.VMEM((members, full, cols), BF16),
            pltpu.VMEM((members, full, cols), BF16),
            pltpu.VMEM((outn * rows, cols), F32),
            pltpu.VMEM((members, 3 * full, cols), BF16),
            pltpu.VMEM((members, 6 * chans, cols), BF16),
            pltpu.VMEM((members, cols // lane, full, lane), F32),
            pltpu.VMEM((members, full, cols), BF16),
            pltpu.VMEM((members, 2, chans, cols), BF16),
            pltpu.VMEM((members, 2, chans, cols), BF16),
            pltpu.VMEM((members, 2, chans, cols), F32),
            pltpu.VMEM((members, 2, chans, cols), BF16),
            pltpu.VMEM((members, 2, outn * rows, cols), BF16),
            pltpu.VMEM((members, outn * rows, cols), F32),
            pltpu.VMEM((members, outn * rows, cols), BF16),
            pltpu.VMEM((peers, members, outn * rows, cols), BF16),
            pltpu.VMEM((members, outn * rows, cols), BF16),
            pltpu.VMEM((members, 2, chans, cols), F32),
            pltpu.VMEM((2 * chans, outn * rows), BF16),
            pltpu.VMEM((full, 3 * full), BF16),
            pltpu.VMEM((full, 6 * chans), BF16),
            pltpu.VMEM((full, 3 * full), BF16),
            pltpu.VMEM((full, 6 * chans), BF16),
            pltpu.VMEM((outn * rows, full), BF16),
            pltpu.VMEM((full, outn * rows), BF16),
            pltpu.VMEM((2 * chans, full), BF16),
            dma((2 * members + 1,)),
            dma((members, 2)),
            dma((members, 2)),
            dma((members, 2)),
            dma((members, 2)),
            dma((members, 2, peers)),
            dma((members, 2, peers)),
            dma((members, 2)),
            dma((members, 2)),
        ],
        compiler_params=pltpu.CompilerParams(collective_id=0, has_side_effects=True, vmem_limit_bytes=58 * 2**20),
    )(
        features.reshape(members, full, cols),
        skip.reshape(members, full, cols),
        conv_weight,
        out_weight,
        target.reshape(outn * rows, cols),
    )
    return result.reshape(members, chans, rows, cols)


def solution(mesh):
    placed = (
        P("member", None, "space", None),
        P("member", None, "space", None),
        P(),
        P(),
        P(None, "space", None),
    )
    return jax.shard_map(
        local,
        mesh=mesh,
        in_specs=placed,
        out_specs=P("member", None, "space", None),
        check_vma=False,
    )
```
